128 devices in a mesh: dp: 4 (over x), expert: 16 (over z, y), etp: 2 (over core).
Axes of the slice: x: 4, y: 4, z: 4, core: 2. Of those that a mesh axis runs over, the one named last changes fastest.
Arguments:
- grad_out: bfloat16 [8192, 4096], P(('dp', 'expert'), 'etp'), may hold values from -6 to 6
- routes: int32 [8192, 8], P(('dp', 'expert')), may hold values from 0 to 31, all different within a row; in each aligned block of 128 rows (0 to 127, 128 to 255, ...) at most 64 rows name the same one
- gate_probs: bfloat16 [8192, 8], P(('dp', 'expert')), may hold values from 0.019897461 to 0.5
- hidden_saved: bfloat16 [4, 32, 1024, 1536], P('dp', 'expert', None, 'etp'), may hold values from -0.29882812 to 0.29882812
- down_weight: bfloat16 [32, 1536, 4096], P('expert', 'etp'), may hold values from -0.15625 to 0.15625
Outputs:
- grad_hidden: bfloat16 [4, 32, 1024, 1536], P('dp', 'expert', None, 'etp')
- grad_weight: bfloat16 [4096, 32, 1536], P('dp', 'expert', 'etp')
- grad_probs: float32 [8192, 8], P(('dp', 'expert'))
The draws below stay inside these ranges and needn't reach their ends.
Inputs may be any that keep to these rules, and one draw needn't show every extreme that they name: `routes`: each row names 8 different experts. Among the 128 rows of one block of consecutive rows no expert is named more than 64 times, and in every draw some expert is named exactly 64 times in some block.
All inputs are finite; a program needn't handle non-finite values.
Results may differ from the reference program's by a relative error of at most 0.013.
Values may be sent and summed in bfloat16 or wider, within the bound.
No kernel may reach another device: no remote copies, remote signals or barrier semaphores. Data moves between devices by JAX's collectives and lax.ppermute only.
A program may use at most 128 MiB of HBM per device.

```python
import math
import jax
import jax.numpy as jnp
import numpy as np
from jax import lax

D = 4096
FF = 1536
TOP = 8
EXPERTS = 32
TOK_DEV = 128
CAP = 64
SLOTS = 1024
TOKENS = 8192
N_DP = 4
N_EXPERT = 16


def block_levels(rng, shape, shards, least, high):
    def one(axis_at, parts):
        heights = jax.random.uniform(jax.random.fold_in(jax.random.fold_in(rng, 6), axis_at), (parts,), jnp.float32, least / len(shards), high / len(shards))
        return jnp.repeat(jnp.exp(heights), shape[axis_at] // parts).reshape((-1,) + (1,) * (len(shape) - axis_at - 1))

    factor_of = one(*shards[0])
    for cut in shards[1:]:
        factor_of = factor_of * one(*cut)
    return factor_of


def assign_block(key, own, number, rows, count, top, most, skew):
    ranking = jax.random.permutation(key, count)
    heavy_load, usual = shares(count, rows * top, most, skew, True), shares(count, rows * top, most, skew, False)
    places = jnp.arange(count)

    def named(tallies, turn):
        used = int((tallies > 0).sum())
        fixed = max(1, used // 4)
        passed = fixed + (places - fixed + turn * (used - fixed)) % max(1, count - fixed)
        return jnp.zeros((count,), jnp.int32).at[ranking[jnp.where(places < fixed, places, passed)]].set(jnp.asarray(tallies, jnp.int32))

    tallies = jnp.where(number % 4 == 0, named(heavy_load, number // 4), named(usual, number - number // 4 - 1))
    mixed = jax.random.permutation(jax.random.fold_in(own, 3), count)
    giver, receiver = mixed[0:count // 2 * 2:2], mixed[1:count // 2 * 2:2]
    room = jnp.minimum(tallies[giver] - 1, most - tallies[receiver]) // 2
    room = jnp.where((giver == ranking[0]) | (receiver == ranking[0]) | (tallies[receiver] == 0), 0, jnp.maximum(room, 0))
    passed = jax.random.randint(jax.random.fold_in(own, 4), (count // 2,), 0, 1 << 20) % (room + 1)
    tallies = tallies.at[giver].add(-passed).at[receiver].add(passed)
    items = jnp.searchsorted(jnp.cumsum(tallies), jnp.arange(rows * top), side="right").astype(jnp.int32)
    listing = items.reshape(top, rows).T
    listing = listing[jax.random.permutation(jax.random.fold_in(own, 1), rows)]
    turn = jax.random.randint(jax.random.fold_in(own, 2), (rows, 1), 0, top)
    return jnp.take_along_axis(listing, (jnp.arange(top)[None, :] + turn) % top, axis=1)


def shares(number_of, total, bound, slope, full):
    loads = [(1 << 20) // math.isqrt(grade ** slope) + 1 for grade in range(1, number_of + 1)]
    largest = bound if full else min(bound, max(-(-total // number_of), total * loads[0] // sum(loads)))
    least = 1 if total - largest >= number_of - 1 else 0
    counts, surplus = [largest] + [least] * (number_of - 1), total - largest - least * (number_of - 1)
    while surplus > 0:
        free = [i for i in range(1, number_of) if counts[i] < largest] or [i for i in range(1, number_of) if counts[i] < bound]
        whole, left = sum([loads[i] for i in free]), surplus
        for i in free:
            more = min(bound - counts[i], max(1, left * loads[i] // whole), surplus)
            counts[i] = counts[i] + more
            surplus = surplus - more
    return np.array(counts)


def gaussian(rng, extent, width, bound, shards=(), held_as=jnp.bfloat16):
    result = width * jax.random.normal(rng, extent, jnp.float32)
    if shards:
        result = result * block_levels(rng, extent, shards, -0.22, 0.18)
    return jnp.clip(result, -bound, bound).astype(held_as)


def setup_inputs(seed: int = 0) -> dict:
    arg_keys = jax.random.split(jax.random.key(seed), 6)
    grad_out = gaussian(arg_keys[0], (TOKENS, D), 1.0, 6.0, ((0, 64), (1, 2)))
    routes_keys = jax.random.split(jax.random.fold_in(arg_keys[1], 1), TOKENS // TOK_DEV)
    routes_turns = jax.random.permutation(jax.random.fold_in(arg_keys[1], 3), TOKENS // TOK_DEV)
    routes = jax.vmap(lambda own, number: assign_block(jax.random.fold_in(arg_keys[1], 2), own, number, TOK_DEV, EXPERTS, TOP, CAP, 2))(routes_keys, routes_turns).reshape((TOKENS, TOP))
    gate_probs = jnp.clip(jnp.exp(math.log(0.5) - 3.224016 * jax.random.uniform(arg_keys[2], (TOKENS, TOP), jnp.float32) ** block_levels(arg_keys[2], (TOKENS, TOP), ((0, 64),), -0.2, 0.2)), 0.019897461, 0.5).astype(jnp.bfloat16)
    hidden_saved = gaussian(arg_keys[3], (N_DP, EXPERTS, SLOTS, FF), 0.05, 0.29882812, ((0, 4), (1, 16), (3, 2)))
    down_weight = gaussian(arg_keys[4], (EXPERTS, FF, D), FF ** -0.5, 0.15625, ((0, 16), (1, 2)))
    return dict(grad_out=grad_out, routes=routes, gate_probs=gate_probs, hidden_saved=hidden_saved, down_weight=down_weight)


def slot_positions(route_block, capacity, experts):
    flat_routes = route_block.reshape(-1).astype(jnp.int32)
    one_hot = (flat_routes[:, None] == jnp.arange(experts, dtype=jnp.int32)[None, :]).astype(jnp.int32)
    before = jnp.cumsum(one_hot, axis=0) - one_hot
    slot_rank = jnp.sum(before * one_hot, axis=1).astype(jnp.int32)
    return (flat_routes * capacity + slot_rank).astype(jnp.int32)


def reference(grad_out, routes, gate_probs, hidden_saved, down_weight):
    blocks = N_DP * N_EXPERT
    route_blocks = routes.reshape(blocks, TOK_DEV, TOP)
    prob_blocks = gate_probs.reshape(blocks, TOK_DEV * TOP).astype(jnp.float32)
    slot_index = jax.vmap(lambda block_routes: slot_positions(block_routes, CAP, EXPERTS))(route_blocks)
    owners = (jnp.arange(blocks, dtype=jnp.int32)[:, None] * TOK_DEV
              + jnp.arange(TOK_DEV * TOP, dtype=jnp.int32)[None, :] // TOP).astype(jnp.int32)

    def token_fill(index_row, owner_row):
        return jnp.full((EXPERTS * CAP,), TOKENS, jnp.int32).at[index_row].set(owner_row)

    def prob_fill(index_row, prob_row):
        return jnp.zeros((EXPERTS * CAP,), jnp.float32).at[index_row].set(prob_row)

    token_table = jax.vmap(token_fill)(slot_index, owners)
    prob_table = jax.vmap(prob_fill)(slot_index, prob_blocks)
    token_table = token_table.reshape(N_DP, N_EXPERT, EXPERTS, CAP).transpose(2, 0, 1, 3).reshape(EXPERTS, N_DP, SLOTS)
    prob_table = prob_table.reshape(N_DP, N_EXPERT, EXPERTS, CAP).transpose(2, 0, 1, 3).reshape(EXPERTS, N_DP, SLOTS)
    padded = jnp.concatenate([grad_out, jnp.zeros((1, D), grad_out.dtype)], axis=0)
    hidden_by_expert = hidden_saved.transpose(1, 0, 2, 3)

    def per_expert(operands):
        weight, tables, probs, hidden = operands
        total = jnp.zeros((D, FF), jnp.float32)
        hidden_list = []
        score_list = []
        for copy in range(N_DP):
            arrived = jnp.take(padded, tables[copy], axis=0)
            weights_col = probs[copy][:, None]
            projected = jnp.dot(arrived, weight.T, preferred_element_type=jnp.float32)
            hidden_list.append((weights_col * projected).astype(jnp.bfloat16))
            score_list.append(jnp.sum(hidden[copy].astype(jnp.float32) * projected, axis=1))
            scaled = (weights_col * arrived.astype(jnp.float32)).astype(jnp.bfloat16)
            term = jnp.dot(scaled.T, hidden[copy], preferred_element_type=jnp.float32).astype(jnp.bfloat16)
            term = lax.optimization_barrier(term)
            total = total + term.astype(jnp.float32)
        return jnp.stack(hidden_list), total.astype(jnp.bfloat16), jnp.stack(score_list)

    grads, weight_grads, scores = lax.map(per_expert, (down_weight, token_table, prob_table, hidden_by_expert))
    grad_hidden = grads.transpose(1, 0, 2, 3)
    grad_weight = weight_grads.transpose(1, 0, 2)
    score_blocks = scores.reshape(EXPERTS, N_DP, N_EXPERT, CAP).transpose(1, 2, 0, 3).reshape(blocks, EXPERTS * CAP)
    grad_probs = jnp.take_along_axis(score_blocks, slot_index, axis=1).reshape(TOKENS, TOP)
    return grad_hidden, grad_weight, grad_probs
```

```python
import functools

import jax
import jax.numpy as jnp
from jax import lax
from jax.experimental import pallas as pl
from jax.experimental.pallas import tpu as pltpu
from jax.sharding import PartitionSpec as P

CAP = 64
BF = jnp.bfloat16
F32 = jnp.float32


def onehot_rows(meta_ref, b, weighted):
    rows = []
    tokens = meta_ref.shape[-1]
    slots = lax.broadcasted_iota(jnp.int32, (CAP, tokens), 0).astype(F32)
    for x in range(2):
        slot = jnp.broadcast_to(meta_ref[b, x : x + 1, :], (CAP, tokens))
        one = jnp.ones((CAP, tokens), F32)
        if weighted:
            one = jnp.broadcast_to(meta_ref[b, 2 + x : 3 + x, :], (CAP, tokens))
        rows.append(jnp.where(slot == slots, one, 0.0))
    return rows


def pair_matrix(blocks):
    zero = jnp.zeros_like(blocks[0][0])
    rows = []
    for x in range(2):
        rows.append(jnp.concatenate([blocks[0][x], zero], axis=1))
        rows.append(jnp.concatenate([zero, blocks[1][x]], axis=1))
    return jnp.concatenate(rows, axis=0).astype(BF)


def projected_kernel(meta_ref, tok_ref, w_ref, h_ref, gh_ref, ts_ref, arr_ref):
    nb, halves, tokens, half = tok_ref.shape
    pieces = 512
    cols = []
    for p in range(nb // 2):
        ones = [onehot_rows(meta_ref, 2 * p + i, False) for i in range(2)]
        weights = [onehot_rows(meta_ref, 2 * p + i, True) for i in range(2)]
        cols.append((ones, weights))
        pick = pair_matrix(ones)
        for h in range(halves):
            for f in range(half // pieces):
                src = tok_ref[2 * p : 2 * p + 2, h, :, f * pieces : (f + 1) * pieces]
                got = jnp.dot(pick, src.reshape(2 * tokens, pieces), preferred_element_type=F32).astype(BF)
                at = h * half + f * pieces
                for x in range(2):
                    arr_ref[x, p * 2 * CAP : (p + 1) * 2 * CAP, at : at + pieces] = got[x * 2 * CAP : (x + 1) * 2 * CAP]
    for x in range(2):
        proj = lax.dot_general(arr_ref[x], w_ref[x], (((1,), (1,)), ((), ())), preferred_element_type=F32)
        for b in range(nb):
            ones, weights = cols[b // 2][0][b % 2][x], cols[b // 2][1][b % 2][x]
            prob = jnp.sum(weights, axis=1, keepdims=True)
            mine = proj[b * CAP : (b + 1) * CAP]
            gh_ref[x, b * CAP : (b + 1) * CAP, :] = (prob * mine).astype(BF)
            score = jnp.sum(h_ref[x, b * CAP : (b + 1) * CAP, :].astype(F32) * mine, axis=1, keepdims=True)
            ts_ref[b, x : x + 1, :] = jnp.sum(ones * score, axis=0, keepdims=True)


def projected_call(meta, tok, w, h):
    blocks, halves, tokens, half = tok.shape
    experts, slots, hid = h.shape
    nb = 4
    rows = nb * CAP
    return pl.pallas_call(
        projected_kernel,
        grid=(blocks // nb,),
        in_specs=[
            pl.BlockSpec((nb, 4, tokens), lambda i: (i, 0, 0)),
            pl.BlockSpec((nb, halves, tokens, half), lambda i: (i, 0, 0, 0)),
            pl.BlockSpec(w.shape, lambda i: (0, 0, 0), pipeline_mode=pl.Buffered(1)),
            pl.BlockSpec((experts, rows, hid), lambda i: (0, i, 0)),
        ],
        out_specs=[
            pl.BlockSpec((experts, rows, hid), lambda i: (0, i, 0)),
            pl.BlockSpec((nb, 2, tokens), lambda i: (i, 0, 0)),
        ],
        out_shape=[
            jax.ShapeDtypeStruct((experts, slots, hid), BF),
            jax.ShapeDtypeStruct((blocks, 2, tokens), F32),
        ],
        scratch_shapes=[pltpu.VMEM((experts, rows, halves * half), BF)],
        compiler_params=pltpu.CompilerParams(vmem_limit_bytes=52 << 20),
        cost_estimate=pl.CostEstimate(flops=17_000_000_000, bytes_accessed=36_000_000, transcendentals=0),
        name="projected",
    )(meta, tok, w, h)


def grad_kernel(nc, first, *refs):
    metas, toks, hids = refs[:nc], refs[nc : 2 * nc], refs[2 * nc : 3 * nc]
    rest = refs[3 * nc :]
    if not first:
        prev_ref, rest = rest[0], rest[1:]
    out_ref, sc_ref = rest
    step = pl.program_id(0)
    nb, halves, tokens, half = toks[0].shape

    @pl.when(step == 0)
    def _():
        out_ref[...] = jnp.zeros_like(out_ref) if first else prev_ref[...]

    for c in range(nc):
        for p in range(nb // 2):
            pick = pair_matrix([onehot_rows(metas[c], 2 * p + i, True) for i in range(2)])
            for h in range(halves):
                src = toks[c][2 * p : 2 * p + 2, h, :, :]
                got = jnp.dot(pick, src.reshape(2 * tokens, half), preferred_element_type=F32).astype(BF)
                for x in range(2):
                    sc_ref[x, p * 2 * CAP : (p + 1) * 2 * CAP, h * half : (h + 1) * half] = got[
                        x * 2 * CAP : (x + 1) * 2 * CAP
                    ]
        for x in range(2):
            out_ref[x] += lax.dot_general(
                sc_ref[x], hids[c][x], (((0,), (0,)), ((), ())), preferred_element_type=F32
            )


def grad_call(metas, toks, hids, prev=None):
    nc = len(metas)
    blocks, halves, tokens, half = toks[0].shape
    experts, slots, hid = hids[0].shape
    nb = 8
    rows = nb * CAP
    feats = halves * half
    acc = jax.ShapeDtypeStruct((experts, feats, hid), F32)
    whole = pl.BlockSpec(acc.shape, lambda i: (0, 0, 0), pipeline_mode=pl.Buffered(1))
    specs = (
        [pl.BlockSpec((nb, 4, tokens), lambda i: (i, 0, 0))] * nc
        + [pl.BlockSpec((nb, halves, tokens, half), lambda i: (i, 0, 0, 0))] * nc
        + [pl.BlockSpec((experts, rows, hid), lambda i: (0, i, 0))] * nc
    )
    args = [*metas, *toks, *hids]
    if prev is not None:
        specs.append(whole)
        args.append(prev)
    return pl.pallas_call(
        functools.partial(grad_kernel, nc, prev is None),
        grid=(blocks // nb,),
        in_specs=specs,
        out_specs=whole,
        out_shape=acc,
        scratch_shapes=[pltpu.VMEM((experts, rows, feats), BF)],
        compiler_params=pltpu.CompilerParams(vmem_limit_bytes=52 << 20),
        cost_estimate=pl.CostEstimate(
            flops=nc * 4_400_000_000, bytes_accessed=nc * 7_500_000 + 12_000_000, transcendentals=0
        ),
        name=f"grad_weight_{nc}",
    )(*args)


def shift(x, axis, by):
    n = lax.axis_size(axis)
    return lax.ppermute(x, axis, [(i, (i + by) % n) for i in range(n)])


def body(grad_out, routes, gate_probs, hidden_saved, down_weight):
    d, e, t = lax.axis_index("dp"), lax.axis_index("expert"), lax.axis_index("etp")
    n_dp, n_ex = lax.axis_size("dp"), lax.axis_size("expert")
    tokens, half = grad_out.shape
    local = down_weight.shape[0]
    own = hidden_saved[0]

    routes_t = routes.T
    packed = jnp.concatenate([routes_t.astype(BF), gate_probs.T], axis=0)
    tables = lax.all_gather(packed, ("dp", "expert"), axis=0)
    named, weight = tables[:, :8], tables[:, 8:].astype(F32)
    before = (jnp.arange(tokens)[:, None] < jnp.arange(tokens)[None, :]).astype(BF)
    slots, probs = [], []
    for x in range(local):
        hit = named == (e * local + x).astype(BF)
        match = jnp.any(hit, axis=1)
        rank = jnp.dot(match.astype(BF), before, preferred_element_type=F32)
        slots.append(jnp.where(match, rank, -1.0))
        probs.append(jnp.sum(jnp.where(hit, weight, 0.0), axis=1))
    meta = jnp.stack(slots + probs, axis=1).reshape(n_dp, n_ex, 2 * local, tokens)

    h_left = shift(own, "dp", 1)
    h_right = shift(own, "dp", -1)
    h_far = jnp.stack([shift(h_left[0], "dp", 1), shift(h_right[1], "dp", -1)])

    other = shift(grad_out, "etp", 1)
    full = jnp.where(t == 0, jnp.concatenate([grad_out, other], 1), jnp.concatenate([other, grad_out], 1))
    part = half // n_dp

    def slice_for(who):
        return lax.dynamic_slice(full, (0, who * (2 * part) + t * part), (tokens, part))

    mine = [slice_for(d)] + [shift(slice_for((d + s) % n_dp), "dp", s) for s in range(1, n_dp)]

    tok = lax.all_gather(grad_out, ("expert", "etp"), axis=0).reshape(n_ex, 2, tokens, half)
    feats = lax.all_gather(jnp.stack(mine), ("expert", "etp"), axis=0).reshape(n_ex, 2, n_dp, tokens, part)

    def meta_of(s):
        return lax.dynamic_index_in_dim(meta, (d - s) % n_dp, 0, keepdims=False)

    grad_hidden, scores = projected_call(meta_of(0), tok, down_weight, own)

    metas = [meta_of(s) for s in range(n_dp)]
    toks = [feats[:, :, s] for s in range(n_dp)]
    near = grad_call([metas[0], metas[1], metas[3]], [toks[0], toks[1], toks[3]], [own, h_left, h_right])
    total = grad_call([metas[2]], [toks[2]], [h_far], near)
    grad_weight = total.astype(BF).transpose(1, 0, 2)

    back = lax.all_to_all(scores, "expert", split_axis=0, concat_axis=0)
    back = back + shift(back, "etp", 1)
    back = back.reshape(1, n_ex * local, tokens)
    experts = jnp.arange(n_ex * local, dtype=jnp.int32)[None, :, None]
    grad_probs = jnp.sum(jnp.where(routes_t[:, None, :] == experts, back, 0.0), axis=1).T
    return grad_hidden[None], grad_weight, grad_probs


def solution(mesh):
    placed = (
        P(("dp", "expert"), "etp"),
        P(("dp", "expert"), None),
        P(("dp", "expert"), None),
        P("dp", "expert", None, "etp"),
        P("expert", "etp", None),
    )
    return jax.shard_map(
        body,
        mesh=mesh,
        in_specs=placed,
        out_specs=(
            P("dp", "expert", None, "etp"),
            P("dp", "expert", "etp"),
            P(("dp", "expert"), None),
        ),
        check_vma=False,
    )
```

```python
import functools

import jax
import jax.numpy as jnp
from jax import lax
from jax.experimental import pallas as pl
from jax.experimental.pallas import tpu as pltpu
from jax.sharding import PartitionSpec as P

CAP = 64
BF = jnp.bfloat16
F32 = jnp.float32
HALF, COL, COPY = 0, 1, 2


def onehot_rows(slot_row, value_row):
    shape = (CAP, slot_row.shape[1])
    slots = lax.broadcasted_iota(jnp.int32, shape, 0).astype(F32)
    value = jnp.ones(shape, F32) if value_row is None else jnp.broadcast_to(value_row, shape)
    return jnp.where(jnp.broadcast_to(slot_row, shape) == slots, value, 0.0)


def slots_kernel(meta_ref, pick_ref):
    for b in range(meta_ref.shape[1]):
        for x in range(2):
            rows = onehot_rows(meta_ref[0, b, x : x + 1, :], meta_ref[0, b, 2 + x : 3 + x, :])
            pick_ref[0, b, x * CAP : (x + 1) * CAP, :] = rows.astype(BF)


def slots_call(meta):
    copies, blocks, _, tokens = meta.shape
    return pl.pallas_call(
        slots_kernel,
        grid=(copies,),
        in_specs=[pl.BlockSpec((1, blocks, 4, tokens), lambda i: (i, 0, 0, 0))],
        out_specs=pl.BlockSpec((1, blocks, 2 * CAP, tokens), lambda i: (i, 0, 0, 0)),
        out_shape=jax.ShapeDtypeStruct((copies, blocks, 2 * CAP, tokens), BF),
        cost_estimate=pl.CostEstimate(flops=10_000_000, bytes_accessed=2_500_000, transcendentals=0),
        name="slots",
    )(meta)


def projected_kernel(tab_ref, meta_ref, tok_ref, w_ref, h_ref, gh_ref, ts_ref, arr_ref):
    nb, halves, tokens, half = tok_ref.shape
    pieces = 1024
    for b in range(nb):
        rows = [onehot_rows(meta_ref[0, b, x : x + 1, :], None) for x in range(2)]
        pick = jnp.concatenate(rows, axis=0).astype(BF)
        for h in range(halves):
            for f in range(half // pieces):
                src = tok_ref[b, h, :, f * pieces : (f + 1) * pieces]
                got = jnp.dot(pick, src, preferred_element_type=F32).astype(BF)
                at = h * half + f * pieces
                for x in range(2):
                    arr_ref[x, b * CAP : (b + 1) * CAP, at : at + pieces] = got[x * CAP : (x + 1) * CAP]
    for x in range(2):
        proj = lax.dot_general(arr_ref[x], w_ref[x], (((1,), (1,)), ((), ())), preferred_element_type=F32)
        for b in range(nb):
            slot_row = meta_ref[0, b, x : x + 1, :]
            ones = onehot_rows(slot_row, None)
            weights = onehot_rows(slot_row, meta_ref[0, b, 2 + x : 3 + x, :])
            prob = jnp.sum(weights, axis=1, keepdims=True)
            mine = proj[b * CAP : (b + 1) * CAP]
            gh_ref[x, b * CAP : (b + 1) * CAP, :] = (prob * mine).astype(BF)
            score = jnp.sum(h_ref[x, b * CAP : (b + 1) * CAP, :].astype(F32) * mine, axis=1, keepdims=True)
            ts_ref[b, x : x + 1, :] = jnp.sum(ones * score, axis=0, keepdims=True)


def projected_call(tab, meta, tok, w, h):
    blocks, halves, tokens, half = tok.shape
    experts, slots, hid = h.shape
    nb = 4
    rows = nb * CAP
    return pl.pallas_call(
        projected_kernel,
        grid_spec=pltpu.PrefetchScalarGridSpec(
            num_scalar_prefetch=1,
            grid=(blocks // nb,),
            in_specs=[
                pl.BlockSpec((1, nb, 4, tokens), lambda i, tab: (tab[COPY], i, 0, 0)),
                pl.BlockSpec((nb, halves, tokens, half), lambda i, tab: (i, 0, 0, 0)),
                pl.BlockSpec(w.shape, lambda i, tab: (0, 0, 0), pipeline_mode=pl.Buffered(1)),
                pl.BlockSpec((experts, rows, hid), lambda i, tab: (0, i, 0)),
            ],
            out_specs=[
                pl.BlockSpec((experts, rows, hid), lambda i, tab: (0, i, 0)),
                pl.BlockSpec((nb, 2, tokens), lambda i, tab: (i, 0, 0)),
            ],
            scratch_shapes=[pltpu.VMEM((experts, rows, halves * half), BF)],
        ),
        out_shape=[
            jax.ShapeDtypeStruct((experts, slots, hid), BF),
            jax.ShapeDtypeStruct((blocks, 2, tokens), F32),
        ],
        compiler_params=pltpu.CompilerParams(vmem_limit_bytes=52 << 20),
        cost_estimate=pl.CostEstimate(flops=17_000_000_000, bytes_accessed=36_000_000, transcendentals=0),
        name="projected",
    )(tab, meta, tok, w, h)


def grad_kernel(first, last, tab_ref, *refs):
    if first:
        nc, (out_ref, sc_ref), refs = 1, refs[-2:], refs[:-2]
    else:
        nc, (prev_ref, out_ref, acc_ref, sc_ref), refs = 3, refs[-4:], refs[:-4]
    picks, tok_refs, hids = refs[:nc], refs[nc : -2 * nc], refs[-2 * nc :]
    acc = out_ref if first else acc_ref
    step = pl.program_id(0)

    @pl.when(step == 0)
    def _():
        acc[...] = jnp.zeros_like(acc) if first else prev_ref[...]

    nb = picks[0].shape[1]
    for c in range(nc):
        for b in range(nb):
            if first:
                halves = [tok_refs[0][b]]
            else:
                halves = [tok_refs[0][b, h, c] for h in range(2)]
            at, row = 0, (c * nb + b) * CAP
            for src in halves:
                got = jnp.dot(picks[c][0, b], src, preferred_element_type=F32).astype(BF)
                for x in range(2):
                    sc_ref[x, row : row + CAP, at : at + src.shape[1]] = got[x * CAP : (x + 1) * CAP]
                at += src.shape[1]
    for x in range(2):
        hid = jnp.concatenate([hids[2 * c + x][0] for c in range(nc)], axis=0)
        acc[x] += lax.dot_general(sc_ref[x], hid, (((0,), (0,)), ((), ())), preferred_element_type=F32)

    if last:

        @pl.when(step == pl.num_programs(0) - 1)
        def _():
            for x in range(2):
                out_ref[:, x, :] = acc[x].astype(BF)


def grad_call(tab, pick, tok, hids, prev=None):
    blocks, tokens = pick.shape[1], pick.shape[3]
    hid = hids[0][0].shape[2]
    nc = len(hids)
    feats = tok.shape[3] // 2 if prev is None else 2 * tok.shape[4]
    nb = 8 if prev is None else 4
    copies = (0,) if prev is None else (1, 2, 3)
    specs = [pl.BlockSpec((1, nb, 2 * CAP, tokens), lambda i, tab, s=s: (tab[COPY + s], i, 0, 0)) for s in copies]
    args = [pick] * nc + [tok]
    if prev is None:
        specs.append(pl.BlockSpec((nb, None, tokens, feats), lambda i, tab: (i, tab[HALF], 0, tab[COL])))
    else:
        specs.append(pl.BlockSpec((nb, 2, nc, tokens, feats // 2), lambda i, tab: (i, 0, 0, 0, 0)))
    for pair in hids:
        for x in range(2):
            at = min(x, pair[x].shape[0] - 1)
            specs.append(pl.BlockSpec((1, nb * CAP, hid), lambda i, tab, at=at: (at, i, 0)))
            args.append(pair[x])
    shape = (2, feats, hid)
    whole = pl.BlockSpec(shape, lambda i, tab: (0, 0, 0), pipeline_mode=pl.Buffered(1))
    outs = (feats, 2, hid)
    out_specs = whole if prev is None else pl.BlockSpec(outs, lambda i, tab: (0, 0, 0), pipeline_mode=pl.Buffered(1))
    scratch = [pltpu.VMEM((2, nc * nb * CAP, feats), BF)]
    if prev is not None:
        specs.append(whole)
        args.append(prev)
        scratch.insert(0, pltpu.VMEM(shape, F32))
    return pl.pallas_call(
        functools.partial(grad_kernel, prev is None, prev is not None),
        grid_spec=pltpu.PrefetchScalarGridSpec(
            num_scalar_prefetch=1, grid=(blocks // nb,), in_specs=specs, out_specs=out_specs, scratch_shapes=scratch
        ),
        out_shape=jax.ShapeDtypeStruct(shape, F32) if prev is None else jax.ShapeDtypeStruct(outs, BF),
        compiler_params=pltpu.CompilerParams(vmem_limit_bytes=52 << 20),
        cost_estimate=pl.CostEstimate(
            flops=nc * 4_400_000_000, bytes_accessed=nc * 7_500_000 + 12_000_000, transcendentals=0
        ),
        name=f"grad_weight_{nc}",
    )(tab, *args)


def shift(x, axis, by):
    n = lax.axis_size(axis)
    return lax.ppermute(x, axis, [(i, (i + by) % n) for i in range(n)])


def body(grad_out, routes, gate_probs, hidden_saved, down_weight):
    d, e, t = lax.axis_index("dp"), lax.axis_index("expert"), lax.axis_index("etp")
    n_dp, n_ex = lax.axis_size("dp"), lax.axis_size("expert")
    tokens, half = grad_out.shape
    local, slots, hid = hidden_saved.shape[1:]
    experts = n_ex * local
    part = half // n_dp
    own = hidden_saved[0]
    tab = jnp.stack([d // 2, d % 2] + [(d - s) % n_dp for s in range(n_dp)]).astype(jnp.int32)

    tok = lax.all_gather(grad_out, ("expert", "etp"), axis=0).reshape(n_ex, 2, tokens, half)

    routes_t = routes.T
    hit = routes_t[None] == jnp.arange(experts, dtype=jnp.int32)[:, None, None]
    match = jnp.any(hit, axis=1)
    before = (jnp.arange(tokens)[:, None] < jnp.arange(tokens)[None, :]).astype(BF)
    rank = jnp.dot(match.astype(BF), before, preferred_element_type=F32)
    slot = jnp.where(match, rank, -1.0).reshape(n_ex, local, tokens)
    prob = jnp.sum(jnp.where(hit, gate_probs.T[None].astype(F32), 0.0), axis=1).reshape(n_ex, local, tokens)
    to_send = jnp.concatenate([slot, prob], axis=1)
    to_send = jnp.broadcast_to(to_send[None], (n_dp, *to_send.shape)).reshape(n_dp * n_ex, 2 * local, tokens)
    meta = lax.all_to_all(to_send, ("dp", "expert"), split_axis=0, concat_axis=0)
    meta = meta.reshape(n_dp, n_ex, 2 * local, tokens)
    meta, rows = lax.optimization_barrier((meta, grad_out))
    own_0, own_1 = lax.optimization_barrier((own[:1], own[1:], meta))[:2]
    left_0, right_1 = shift(own_0, "dp", 1), shift(own_1, "dp", -1)
    left_1, right_0 = shift(own_1, "dp", 1), shift(own_0, "dp", -1)

    other = shift(rows, "etp", 1)
    full = jnp.where(t == 0, jnp.concatenate([grad_out, other], 1), jnp.concatenate([other, grad_out], 1))

    def slice_for(who):
        return lax.dynamic_slice(full, (0, who * (2 * part) + t * part), (tokens, part))

    mine = jnp.stack([shift(slice_for((d + s) % n_dp), "dp", s) for s in range(1, n_dp)])
    feats = lax.all_gather(mine, ("expert", "etp"), axis=0).reshape(n_ex, 2, n_dp - 1, tokens, part)

    h_far = (shift(left_0, "dp", 1), shift(right_1, "dp", -1))

    pick = slots_call(meta)

    grad_hidden, scores = projected_call(tab, meta, tok, down_weight, own)
    total = grad_call(tab, pick, tok, [(own, own)])
    total = grad_call(tab, pick, feats, [(left_0, left_1), h_far, (right_0, right_1)], total)
    grad_weight = total

    back = lax.all_to_all(scores, "expert", split_axis=0, concat_axis=0)
    back = back + shift(back, "etp", 1)
    back = back.reshape(1, experts, tokens)
    numbers = jnp.arange(experts, dtype=jnp.int32)[None, :, None]
    grad_probs = jnp.sum(jnp.where(routes_t[:, None, :] == numbers, back, 0.0), axis=1).T
    return grad_hidden[None], grad_weight, grad_probs


def solution(mesh):
    placed = (
        P(("dp", "expert"), "etp"),
        P(("dp", "expert"), None),
        P(("dp", "expert"), None),
        P("dp", "expert", None, "etp"),
        P("expert", "etp", None),
    )
    return jax.shard_map(
        body,
        mesh=mesh,
        in_specs=placed,
        out_specs=(
            P("dp", "expert", None, "etp"),
            P("dp", "expert", "etp"),
            P(("dp", "expert"), None),
        ),
        check_vma=False,
    )
```

```python
import functools

import jax
import jax.numpy as jnp
from jax import lax
from jax.experimental import pallas as pl
from jax.experimental.pallas import tpu as pltpu
from jax.sharding import PartitionSpec as P

CAP = 64
BF = jnp.bfloat16
F32 = jnp.float32
HALF, COL, COPY = 0, 1, 2


def onehot_rows(slot_row, value_row):
    shape = (CAP, slot_row.shape[1])
    slots = lax.broadcasted_iota(jnp.int32, shape, 0).astype(F32)
    value = jnp.ones(shape, F32) if value_row is None else jnp.broadcast_to(value_row, shape)
    return jnp.where(jnp.broadcast_to(slot_row, shape) == slots, value, 0.0)


def slots_kernel(meta_ref, pick_ref):
    for b in range(meta_ref.shape[1]):
        for x in range(2):
            rows = onehot_rows(meta_ref[0, b, x : x + 1, :], meta_ref[0, b, 2 + x : 3 + x, :])
            pick_ref[0, b, x * CAP : (x + 1) * CAP, :] = rows.astype(BF)


def slots_call(meta):
    copies, blocks, _, tokens = meta.shape
    return pl.pallas_call(
        slots_kernel,
        grid=(copies,),
        in_specs=[pl.BlockSpec((1, blocks, 4, tokens), lambda i: (i, 0, 0, 0))],
        out_specs=pl.BlockSpec((1, blocks, 2 * CAP, tokens), lambda i: (i, 0, 0, 0)),
        out_shape=jax.ShapeDtypeStruct((copies, blocks, 2 * CAP, tokens), BF),
        cost_estimate=pl.CostEstimate(flops=10_000_000, bytes_accessed=2_500_000, transcendentals=0),
        name="slots",
    )(meta)


def projected_kernel(tab_ref, meta_ref, tok_ref, w_ref, h_ref, gh_ref, ts_ref, arr_ref):
    nb, halves, tokens, half = tok_ref.shape
    pieces = 1024
    for b in range(nb):
        rows = [onehot_rows(meta_ref[0, b, x : x + 1, :], None) for x in range(2)]
        pick = jnp.concatenate(rows, axis=0).astype(BF)
        for h in range(halves):
            for f in range(half // pieces):
                src = tok_ref[b, h, :, f * pieces : (f + 1) * pieces]
                got = jnp.dot(pick, src, preferred_element_type=F32).astype(BF)
                at = h * half + f * pieces
                for x in range(2):
                    arr_ref[x, b * CAP : (b + 1) * CAP, at : at + pieces] = got[x * CAP : (x + 1) * CAP]
    for x in range(2):
        proj = lax.dot_general(arr_ref[x], w_ref[x], (((1,), (1,)), ((), ())), preferred_element_type=F32)
        for b in range(nb):
            slot_row = meta_ref[0, b, x : x + 1, :]
            ones = onehot_rows(slot_row, None)
            weights = onehot_rows(slot_row, meta_ref[0, b, 2 + x : 3 + x, :])
            prob = jnp.sum(weights, axis=1, keepdims=True)
            mine = proj[b * CAP : (b + 1) * CAP]
            gh_ref[x, b * CAP : (b + 1) * CAP, :] = (prob * mine).astype(BF)
            score = jnp.sum(h_ref[x, b * CAP : (b + 1) * CAP, :].astype(F32) * mine, axis=1, keepdims=True)
            ts_ref[b, x : x + 1, :] = jnp.sum(ones * score, axis=0, keepdims=True)


def projected_call(tab, meta, tok, w, h):
    blocks, halves, tokens, half = tok.shape
    experts, slots, hid = h.shape
    nb = 4
    rows = nb * CAP
    return pl.pallas_call(
        projected_kernel,
        grid_spec=pltpu.PrefetchScalarGridSpec(
            num_scalar_prefetch=1,
            grid=(blocks // nb,),
            in_specs=[
                pl.BlockSpec((1, nb, 4, tokens), lambda i, tab: (tab[COPY], i, 0, 0)),
                pl.BlockSpec((nb, halves, tokens, half), lambda i, tab: (i, 0, 0, 0)),
                pl.BlockSpec(w.shape, lambda i, tab: (0, 0, 0), pipeline_mode=pl.Buffered(1)),
                pl.BlockSpec((experts, rows, hid), lambda i, tab: (0, i, 0)),
            ],
            out_specs=[
                pl.BlockSpec((experts, rows, hid), lambda i, tab: (0, i, 0)),
                pl.BlockSpec((nb, 2, tokens), lambda i, tab: (i, 0, 0)),
            ],
            scratch_shapes=[pltpu.VMEM((experts, rows, halves * half), BF)],
        ),
        out_shape=[
            jax.ShapeDtypeStruct((experts, slots, hid), BF),
            jax.ShapeDtypeStruct((blocks, 2, tokens), F32),
        ],
        compiler_params=pltpu.CompilerParams(vmem_limit_bytes=52 << 20),
        cost_estimate=pl.CostEstimate(flops=17_000_000_000, bytes_accessed=36_000_000, transcendentals=0),
        name="projected",
    )(tab, meta, tok, w, h)


def grad_kernel(nc, halves, first, tab_ref, *refs):
    picks, tok_ref, hids, rest = refs[:nc], refs[nc], refs[nc + 1 : 3 * nc + 1], refs[3 * nc + 1 :]
    if first:
        out_ref, acc_ref, sc_ref = rest
    else:
        prev_ref, out_ref, acc_ref, sc_ref, held_ref, sem = rest
        before = pltpu.make_async_copy(prev_ref, held_ref, sem)
    step, steps = pl.program_id(0), pl.num_programs(0)
    nb = picks[0].shape[1]
    group = sc_ref.shape[1] // (nc * nb * CAP)
    turn = lax.rem(step, group)
    if not first:

        @pl.when(step == 0)
        def _():
            before.start()

    for c in range(nc):
        for b in range(nb):
            at = 0
            row = pl.multiple_of((c * group + turn) * nb * CAP, CAP) + b * CAP
            for src in [tok_ref[b]] if halves == 1 else [tok_ref[b, h, c] for h in range(halves)]:
                got = jnp.dot(picks[c][0, b], src, preferred_element_type=F32).astype(BF)
                for x in range(2):
                    sc_ref[x, pl.ds(pl.multiple_of(row, CAP), CAP), at : at + src.shape[1]] = got[x * CAP : (x + 1) * CAP]
                at += src.shape[1]

    def add(place):
        for x in range(2):
            hid = jnp.concatenate([hids[2 * c + x][0] for c in range(nc)], axis=0)
            for f in range(0, sc_ref.shape[2], 512):
                got = lax.dot_general(
                    sc_ref[x, :, f : f + 512], hid, (((0,), (0,)), ((), ())), preferred_element_type=F32
                )
                place(x, slice(f, f + 512), got)

    def keep(x, rows, got):
        acc_ref[x, rows, :] = got

    def more(x, rows, got):
        acc_ref[x, rows, :] += got

    def give(x, rows, got):
        total = acc_ref[x, rows, :] + got
        if first:
            out_ref[x, rows, :] = total.astype(BF)
        else:
            out_ref[rows, x, :] = (total + held_ref[x, rows, :].astype(F32)).astype(BF)

    @pl.when(step == group - 1)
    def _():
        add(keep)

    @pl.when((turn == group - 1) & (step > group - 1) & (step < steps - 1))
    def _():
        add(more)

    @pl.when(step == steps - 1)
    def _():
        if not first:
            before.wait()
        add(give)


def grad_call(tab, pick, tok, hids, prev=None):
    blocks, tokens = pick.shape[1], pick.shape[3]
    hid = hids[0][0].shape[2]
    nc, first = len(hids), prev is None
    feats = tok.shape[3] // 2 if first else 2 * tok.shape[4]
    nb, group = (4, 2) if first else (4, 1)
    copies = (0,) if first else (1, 2, 3)
    specs = [pl.BlockSpec((1, nb, 2 * CAP, tokens), lambda i, tab, s=s: (tab[COPY + s], i, 0, 0)) for s in copies]
    args = [pick] * nc + [tok]
    if first:
        specs.append(pl.BlockSpec((nb, None, tokens, feats), lambda i, tab: (i, tab[HALF], 0, tab[COL])))
    else:
        specs.append(pl.BlockSpec((nb, 2, nc, tokens, feats // 2), lambda i, tab: (i, 0, 0, 0, 0)))
    for pair in hids:
        for x in range(2):
            at = min(x, pair[x].shape[0] - 1)
            specs.append(pl.BlockSpec((1, group * nb * CAP, hid), lambda i, tab, at=at: (at, i // group, 0)))
            args.append(pair[x])
    shape = (2, feats, hid)
    outs = shape if first else (feats, 2, hid)
    scratch = [pltpu.VMEM(shape, F32), pltpu.VMEM((2, nc * group * nb * CAP, feats), BF)]
    if not first:
        specs.append(pl.BlockSpec(memory_space=pl.ANY))
        args.append(prev)
        scratch += [pltpu.VMEM(shape, BF), pltpu.SemaphoreType.DMA]
    return pl.pallas_call(
        functools.partial(grad_kernel, nc, 1 if first else 2, first),
        grid_spec=pltpu.PrefetchScalarGridSpec(
            num_scalar_prefetch=1,
            grid=(blocks // nb,),
            in_specs=specs,
            out_specs=pl.BlockSpec(outs, lambda i, tab: (0, 0, 0), pipeline_mode=pl.Buffered(1)),
            scratch_shapes=scratch,
        ),
        out_shape=jax.ShapeDtypeStruct(outs, BF),
        compiler_params=pltpu.CompilerParams(vmem_limit_bytes=52 << 20),
        cost_estimate=pl.CostEstimate(
            flops=nc * 4_400_000_000, bytes_accessed=nc * 7_500_000 + 6_000_000, transcendentals=0
        ),
        name=f"grad_weight_{nc}",
    )(tab, *args)


def shift(x, axis, by):
    n = lax.axis_size(axis)
    return lax.ppermute(x, axis, [(i, (i + by) % n) for i in range(n)])


def body(grad_out, routes, gate_probs, hidden_saved, down_weight):
    d, e, t = lax.axis_index("dp"), lax.axis_index("expert"), lax.axis_index("etp")
    n_dp, n_ex = lax.axis_size("dp"), lax.axis_size("expert")
    tokens, half = grad_out.shape
    local, slots, hid = hidden_saved.shape[1:]
    experts = n_ex * local
    part = half // n_dp
    own = hidden_saved[0]
    tab = jnp.stack([d // 2, d % 2] + [(d - s) % n_dp for s in range(n_dp)]).astype(jnp.int32)

    tok = lax.all_gather(grad_out, ("expert", "etp"), axis=0).reshape(n_ex, 2, tokens, half)

    routes_t = routes.T
    hit = routes_t[None] == jnp.arange(experts, dtype=jnp.int32)[:, None, None]
    match = jnp.any(hit, axis=1)
    before = (jnp.arange(tokens)[:, None] < jnp.arange(tokens)[None, :]).astype(BF)
    rank = jnp.dot(match.astype(BF), before, preferred_element_type=F32)
    slot = jnp.where(match, rank, -1.0).reshape(n_ex, local, tokens)
    prob = jnp.sum(jnp.where(hit, gate_probs.T[None].astype(F32), 0.0), axis=1).reshape(n_ex, local, tokens)
    to_send = jnp.concatenate([slot, prob], axis=1)
    to_send = jnp.broadcast_to(to_send[None], (n_dp, *to_send.shape)).reshape(n_dp * n_ex, 2 * local, tokens)
    meta = lax.all_to_all(to_send, ("dp", "expert"), split_axis=0, concat_axis=0)
    meta = meta.reshape(n_dp, n_ex, 2 * local, tokens)
    meta, rows = lax.optimization_barrier((meta, grad_out))
    own_0, own_1 = lax.optimization_barrier((own[:1], own[1:], meta))[:2]
    left_0, right_1 = shift(own_0, "dp", 1), shift(own_1, "dp", -1)
    left_1, right_0 = shift(own_1, "dp", 1), shift(own_0, "dp", -1)

    other = shift(rows, "etp", 1)
    full = jnp.where(t == 0, jnp.concatenate([grad_out, other], 1), jnp.concatenate([other, grad_out], 1))

    def slice_for(who):
        return lax.dynamic_slice(full, (0, who * (2 * part) + t * part), (tokens, part))

    mine = jnp.stack([shift(slice_for((d + s) % n_dp), "dp", s) for s in range(1, n_dp)])
    feats = lax.all_gather(mine, ("expert", "etp"), axis=0).reshape(n_ex, 2, n_dp - 1, tokens, part)

    h_far = (shift(left_0, "dp", 1), shift(right_1, "dp", -1))

    pick = slots_call(meta)

    grad_hidden, scores = projected_call(tab, meta, tok, down_weight, own)
    total = grad_call(tab, pick, tok, [(own, own)])
    total = grad_call(tab, pick, feats, [(left_0, left_1), h_far, (right_0, right_1)], total)
    grad_weight = total

    back = lax.all_to_all(scores, "expert", split_axis=0, concat_axis=0)
    back = back + shift(back, "etp", 1)
    back = back.reshape(1, experts, tokens)
    numbers = jnp.arange(experts, dtype=jnp.int32)[None, :, None]
    grad_probs = jnp.sum(jnp.where(routes_t[:, None, :] == numbers, back, 0.0), axis=1).T
    return grad_hidden[None], grad_weight, grad_probs


def solution(mesh):
    placed = (
        P(("dp", "expert"), "etp"),
        P(("dp", "expert"), None),
        P(("dp", "expert"), None),
        P("dp", "expert", None, "etp"),
        P("expert", "etp", None),
    )
    return jax.shard_map(
        body,
        mesh=mesh,
        in_specs=placed,
        out_specs=(
            P("dp", "expert", None, "etp"),
            P("dp", "expert", "etp"),
            P(("dp", "expert"), None),
        ),
        check_vma=False,
    )
```

```python
import functools

import jax
import jax.numpy as jnp
from jax import lax
from jax.experimental import pallas as pl
from jax.experimental.pallas import tpu as pltpu
from jax.sharding import PartitionSpec as P

CAP = 64
BF = jnp.bfloat16
F32 = jnp.float32
HALF, COL, COPY = 0, 1, 2


def onehot_rows(slot_row, value_row):
    shape = (CAP, slot_row.shape[1])
    slots = lax.broadcasted_iota(jnp.int32, shape, 0).astype(F32)
    value = jnp.ones(shape, F32) if value_row is None else jnp.broadcast_to(value_row, shape)
    return jnp.where(jnp.broadcast_to(slot_row, shape) == slots, value, 0.0)


def slots_kernel(meta_ref, pick_ref):
    for b in range(meta_ref.shape[1]):
        for x in range(2):
            rows = onehot_rows(meta_ref[0, b, x : x + 1, :], meta_ref[0, b, 2 + x : 3 + x, :])
            pick_ref[0, b, x * CAP : (x + 1) * CAP, :] = rows.astype(BF)


def slots_call(meta):
    copies, blocks, _, tokens = meta.shape
    return pl.pallas_call(
        slots_kernel,
        grid=(copies,),
        in_specs=[pl.BlockSpec((1, blocks, 4, tokens), lambda i: (i, 0, 0, 0))],
        out_specs=pl.BlockSpec((1, blocks, 2 * CAP, tokens), lambda i: (i, 0, 0, 0)),
        out_shape=jax.ShapeDtypeStruct((copies, blocks, 2 * CAP, tokens), BF),
        cost_estimate=pl.CostEstimate(flops=10_000_000, bytes_accessed=2_500_000, transcendentals=0),
        name="slots",
    )(meta)


def projected_kernel(tab_ref, meta_ref, tok_ref, w_ref, h_ref, gh_ref, ts_ref, arr_ref):
    nb, halves, tokens, half = tok_ref.shape
    pieces = 1024
    for b in range(nb):
        rows = [onehot_rows(meta_ref[0, b, x : x + 1, :], None) for x in range(2)]
        pick = jnp.concatenate(rows, axis=0).astype(BF)
        for h in range(halves):
            for f in range(half // pieces):
                src = tok_ref[b, h, :, f * pieces : (f + 1) * pieces]
                got = jnp.dot(pick, src, preferred_element_type=F32).astype(BF)
                at = h * half + f * pieces
                for x in range(2):
                    arr_ref[x, b * CAP : (b + 1) * CAP, at : at + pieces] = got[x * CAP : (x + 1) * CAP]
    for x in range(2):
        proj = lax.dot_general(arr_ref[x], w_ref[x], (((1,), (1,)), ((), ())), preferred_element_type=F32)
        for b in range(nb):
            slot_row = meta_ref[0, b, x : x + 1, :]
            ones = onehot_rows(slot_row, None)
            weights = onehot_rows(slot_row, meta_ref[0, b, 2 + x : 3 + x, :])
            prob = jnp.sum(weights, axis=1, keepdims=True)
            mine = proj[b * CAP : (b + 1) * CAP]
            gh_ref[x, b * CAP : (b + 1) * CAP, :] = (prob * mine).astype(BF)
            score = jnp.sum(h_ref[x, b * CAP : (b + 1) * CAP, :].astype(F32) * mine, axis=1, keepdims=True)
            ts_ref[b, x : x + 1, :] = jnp.sum(ones * score, axis=0, keepdims=True)


def projected_call(tab, meta, tok, w, h):
    blocks, halves, tokens, half = tok.shape
    experts, slots, hid = h.shape
    nb = 4
    rows = nb * CAP
    return pl.pallas_call(
        projected_kernel,
        grid_spec=pltpu.PrefetchScalarGridSpec(
            num_scalar_prefetch=1,
            grid=(blocks // nb,),
            in_specs=[
                pl.BlockSpec((1, nb, 4, tokens), lambda i, tab: (tab[COPY], i, 0, 0)),
                pl.BlockSpec((nb, halves, tokens, half), lambda i, tab: (i, 0, 0, 0)),
                pl.BlockSpec(w.shape, lambda i, tab: (0, 0, 0), pipeline_mode=pl.Buffered(1)),
                pl.BlockSpec((experts, rows, hid), lambda i, tab: (0, i, 0)),
            ],
            out_specs=[
                pl.BlockSpec((experts, rows, hid), lambda i, tab: (0, i, 0)),
                pl.BlockSpec((nb, 2, tokens), lambda i, tab: (i, 0, 0)),
            ],
            scratch_shapes=[pltpu.VMEM((experts, rows, halves * half), BF)],
        ),
        out_shape=[
            jax.ShapeDtypeStruct((experts, slots, hid), BF),
            jax.ShapeDtypeStruct((blocks, 2, tokens), F32),
        ],
        compiler_params=pltpu.CompilerParams(vmem_limit_bytes=52 << 20),
        cost_estimate=pl.CostEstimate(flops=17_000_000_000, bytes_accessed=36_000_000, transcendentals=0),
        name="projected",
    )(tab, meta, tok, w, h)


def grad_kernel(nc, halves, first, tab_ref, *refs):
    picks, tok_ref, hids, rest = refs[:nc], refs[nc], refs[nc + 1 : 3 * nc + 1], refs[3 * nc + 1 :]
    if first:
        out_ref, acc_ref, sc_ref = rest
    else:
        prev_ref, out_ref, acc_ref, sc_ref, held_ref, sem = rest
        before = pltpu.make_async_copy(prev_ref, held_ref, sem)
    step, steps = pl.program_id(0), pl.num_programs(0)
    nb = picks[0].shape[1]
    group = sc_ref.shape[1] // (nc * nb * CAP)
    turn = lax.rem(step, group)
    if not first:

        @pl.when(step == 0)
        def _():
            before.start()

    for c in range(nc):
        for b in range(nb):
            at = 0
            row = pl.multiple_of((c * group + turn) * nb * CAP, CAP) + b * CAP
            for src in [tok_ref[b]] if halves == 1 else [tok_ref[b, h, c] for h in range(halves)]:
                got = jnp.dot(picks[c][0, b], src, preferred_element_type=F32).astype(BF)
                for x in range(2):
                    sc_ref[x, pl.ds(pl.multiple_of(row, CAP), CAP), at : at + src.shape[1]] = got[x * CAP : (x + 1) * CAP]
                at += src.shape[1]

    def add(place):
        for x in range(2):
            hid = jnp.concatenate([hids[2 * c + x][0] for c in range(nc)], axis=0)
            for f in range(0, sc_ref.shape[2], 512):
                got = lax.dot_general(
                    sc_ref[x, :, f : f + 512], hid, (((0,), (0,)), ((), ())), preferred_element_type=F32
                )
                place(x, slice(f, f + 512), got)

    def keep(x, rows, got):
        acc_ref[x, rows, :] = got

    def more(x, rows, got):
        acc_ref[x, rows, :] += got

    def give(x, rows, got):
        total = acc_ref[x, rows, :] + got
        if first:
            out_ref[x, rows, :] = total.astype(BF)
        else:
            out_ref[rows, x, :] = (total + held_ref[x, rows, :].astype(F32)).astype(BF)

    @pl.when(step == group - 1)
    def _():
        add(keep)

    @pl.when((turn == group - 1) & (step > group - 1) & (step < steps - 1))
    def _():
        add(more)

    @pl.when(step == steps - 1)
    def _():
        if not first:
            before.wait()
        add(give)


def grad_call(tab, pick, tok, hids, prev=None):
    blocks, tokens = pick.shape[1], pick.shape[3]
    hid = hids[0][0].shape[2]
    nc, first = len(hids), prev is None
    feats = tok.shape[3] // 2 if first else 2 * tok.shape[4]
    nb, group = (4, 2) if first else (4, 1)
    copies = (0,) if first else (1, 2, 3)
    specs = [pl.BlockSpec((1, nb, 2 * CAP, tokens), lambda i, tab, s=s: (tab[COPY + s], i, 0, 0)) for s in copies]
    args = [pick] * nc + [tok]
    if first:
        specs.append(pl.BlockSpec((nb, None, tokens, feats), lambda i, tab: (i, tab[HALF], 0, tab[COL])))
    else:
        specs.append(pl.BlockSpec((nb, 2, nc, tokens, feats // 2), lambda i, tab: (i, 0, 0, 0, 0)))
    for pair in hids:
        for x in range(2):
            at = min(x, pair[x].shape[0] - 1)
            specs.append(pl.BlockSpec((1, group * nb * CAP, hid), lambda i, tab, at=at: (at, i // group, 0)))
            args.append(pair[x])
    shape = (2, feats, hid)
    outs = shape if first else (feats, 2, hid)
    scratch = [pltpu.VMEM(shape, F32), pltpu.VMEM((2, nc * group * nb * CAP, feats), BF)]
    if not first:
        specs.append(pl.BlockSpec(memory_space=pl.ANY))
        args.append(prev)
        scratch += [pltpu.VMEM(shape, BF), pltpu.SemaphoreType.DMA]
    return pl.pallas_call(
        functools.partial(grad_kernel, nc, 1 if first else 2, first),
        grid_spec=pltpu.PrefetchScalarGridSpec(
            num_scalar_prefetch=1,
            grid=(blocks // nb,),
            in_specs=specs,
            out_specs=pl.BlockSpec(outs, lambda i, tab: (0, 0, 0), pipeline_mode=pl.Buffered(1)),
            scratch_shapes=scratch,
        ),
        out_shape=jax.ShapeDtypeStruct(outs, BF),
        compiler_params=pltpu.CompilerParams(vmem_limit_bytes=52 << 20),
        cost_estimate=pl.CostEstimate(
            flops=nc * 4_400_000_000, bytes_accessed=nc * 7_500_000 + 6_000_000, transcendentals=0
        ),
        name=f"grad_weight_{nc}",
    )(tab, *args)


def shift(x, axis, by):
    n = lax.axis_size(axis)
    return lax.ppermute(x, axis, [(i, (i + by) % n) for i in range(n)])


def body(grad_out, routes, gate_probs, hidden_saved, down_weight):
    d, e, t = lax.axis_index("dp"), lax.axis_index("expert"), lax.axis_index("etp")
    n_dp, n_ex = lax.axis_size("dp"), lax.axis_size("expert")
    tokens, half = grad_out.shape
    local, slots, hid = hidden_saved.shape[1:]
    experts = n_ex * local
    part = half // n_dp
    own = hidden_saved[0]
    tab = jnp.stack([d // 2, d % 2] + [(d - s) % n_dp for s in range(n_dp)]).astype(jnp.int32)

    tok = lax.all_gather(grad_out, ("expert", "etp"), axis=0).reshape(n_ex, 2, tokens, half)

    other = shift(grad_out, "etp", 1)
    full = jnp.where(t == 0, jnp.concatenate([grad_out, other], 1), jnp.concatenate([other, grad_out], 1))

    def slice_for(who):
        return lax.dynamic_slice(full, (0, who * (2 * part) + t * part), (tokens, part))

    cuts = [slice_for((d + s) % n_dp) for s in range(1, n_dp)]
    routes_t = routes.T
    hit = routes_t[None] == jnp.arange(experts, dtype=jnp.int32)[:, None, None]
    match = jnp.any(hit, axis=1)
    before = (jnp.arange(tokens)[:, None] < jnp.arange(tokens)[None, :]).astype(BF)
    rank = jnp.dot(match.astype(BF), before, preferred_element_type=F32)
    slot = jnp.where(match, rank, -1.0).reshape(n_ex, local, tokens)
    prob = jnp.sum(jnp.where(hit, gate_probs.T[None].astype(F32), 0.0), axis=1).reshape(n_ex, local, tokens)
    to_send = jnp.concatenate([slot, prob], axis=1)
    to_send = jnp.broadcast_to(to_send[None], (n_dp, *to_send.shape)).reshape(n_dp * n_ex, 2 * local, tokens)
    to_send, *cuts = lax.optimization_barrier((to_send, *cuts))
    meta = lax.all_to_all(to_send, ("dp", "expert"), split_axis=0, concat_axis=0)
    meta = meta.reshape(n_dp, n_ex, 2 * local, tokens)
    mine = [shift(cut, "dp", s + 1) for s, cut in enumerate(cuts)]

    own_0, own_1 = lax.optimization_barrier((own[:1], own[1:], meta, *mine))[:2]
    left_0, right_1 = shift(own_0, "dp", 1), shift(own_1, "dp", -1)
    left_1, right_0 = shift(own_1, "dp", 1), shift(own_0, "dp", -1)

    feats = lax.all_gather(jnp.stack(mine), ("expert", "etp"), axis=0).reshape(n_ex, 2, n_dp - 1, tokens, part)

    h_far = (shift(left_0, "dp", 1), shift(right_1, "dp", -1))

    pick = slots_call(meta)

    grad_hidden, scores = projected_call(tab, meta, tok, down_weight, own)
    total = grad_call(tab, pick, tok, [(own, own)])
    total = grad_call(tab, pick, feats, [(left_0, left_1), h_far, (right_0, right_1)], total)
    grad_weight = total

    back = lax.all_to_all(scores, "expert", split_axis=0, concat_axis=0)
    back = back + shift(back, "etp", 1)
    back = back.reshape(1, experts, tokens)
    numbers = jnp.arange(experts, dtype=jnp.int32)[None, :, None]
    grad_probs = jnp.sum(jnp.where(routes_t[:, None, :] == numbers, back, 0.0), axis=1).T
    return grad_hidden[None], grad_weight, grad_probs


def solution(mesh):
    placed = (
        P(("dp", "expert"), "etp"),
        P(("dp", "expert"), None),
        P(("dp", "expert"), None),
        P("dp", "expert", None, "etp"),
        P("expert", "etp", None),
    )
    return jax.shard_map(
        body,
        mesh=mesh,
        in_specs=placed,
        out_specs=(
            P("dp", "expert", None, "etp"),
            P("dp", "expert", "etp"),
            P(("dp", "expert"), None),
        ),
        check_vma=False,
    )
```

```python
import functools

import jax
import jax.numpy as jnp
from jax import lax
from jax.experimental import pallas as pl
from jax.experimental.pallas import tpu as pltpu
from jax.sharding import PartitionSpec as P

CAP = 64
BF = jnp.bfloat16
F32 = jnp.float32
HALF, COL, COPY = 0, 1, 2


def onehot_rows(slot_row, value_row):
    shape = (CAP, slot_row.shape[1])
    slots = lax.broadcasted_iota(jnp.int32, shape, 0).astype(F32)
    value = jnp.ones(shape, F32) if value_row is None else jnp.broadcast_to(value_row, shape)
    return jnp.where(jnp.broadcast_to(slot_row, shape) == slots, value, 0.0)


def slots_kernel(meta_ref, pick_ref):
    for b in range(meta_ref.shape[1]):
        for x in range(2):
            rows = onehot_rows(meta_ref[0, b, x : x + 1, :], meta_ref[0, b, 2 + x : 3 + x, :])
            pick_ref[0, b, x * CAP : (x + 1) * CAP, :] = rows.astype(BF)


def slots_call(meta):
    copies, blocks, _, tokens = meta.shape
    return pl.pallas_call(
        slots_kernel,
        grid=(copies,),
        in_specs=[pl.BlockSpec((1, blocks, 4, tokens), lambda i: (i, 0, 0, 0))],
        out_specs=pl.BlockSpec((1, blocks, 2 * CAP, tokens), lambda i: (i, 0, 0, 0)),
        out_shape=jax.ShapeDtypeStruct((copies, blocks, 2 * CAP, tokens), BF),
        cost_estimate=pl.CostEstimate(flops=10_000_000, bytes_accessed=2_500_000, transcendentals=0),
        name="slots",
    )(meta)


def projected_kernel(tab_ref, meta_ref, tok_ref, w_ref, h_ref, gh_ref, ts_ref, arr_ref):
    nb, halves, tokens, half = tok_ref.shape
    pieces = 1024
    for b in range(nb):
        rows = [onehot_rows(meta_ref[0, b, x : x + 1, :], None) for x in range(2)]
        pick = jnp.concatenate(rows, axis=0).astype(BF)
        for h in range(halves):
            for f in range(half // pieces):
                src = tok_ref[b, h, :, f * pieces : (f + 1) * pieces]
                got = jnp.dot(pick, src, preferred_element_type=F32).astype(BF)
                at = h * half + f * pieces
                for x in range(2):
                    arr_ref[x, b * CAP : (b + 1) * CAP, at : at + pieces] = got[x * CAP : (x + 1) * CAP]
    for x in range(2):
        proj = lax.dot_general(arr_ref[x], w_ref[x], (((1,), (1,)), ((), ())), preferred_element_type=F32)
        for b in range(nb):
            slot_row = meta_ref[0, b, x : x + 1, :]
            ones = onehot_rows(slot_row, None)
            weights = onehot_rows(slot_row, meta_ref[0, b, 2 + x : 3 + x, :])
            prob = jnp.sum(weights, axis=1, keepdims=True)
            mine = proj[b * CAP : (b + 1) * CAP]
            gh_ref[x, b * CAP : (b + 1) * CAP, :] = (prob * mine).astype(BF)
            score = jnp.sum(h_ref[x, b * CAP : (b + 1) * CAP, :].astype(F32) * mine, axis=1, keepdims=True)
            ts_ref[b, x : x + 1, :] = jnp.sum(ones * score, axis=0, keepdims=True)


def projected_call(tab, meta, tok, w, h):
    blocks, halves, tokens, half = tok.shape
    experts, slots, hid = h.shape
    nb = 4
    rows = nb * CAP
    return pl.pallas_call(
        projected_kernel,
        grid_spec=pltpu.PrefetchScalarGridSpec(
            num_scalar_prefetch=1,
            grid=(blocks // nb,),
            in_specs=[
                pl.BlockSpec((1, nb, 4, tokens), lambda i, tab: (tab[COPY], i, 0, 0)),
                pl.BlockSpec((nb, halves, tokens, half), lambda i, tab: (i, 0, 0, 0)),
                pl.BlockSpec(w.shape, lambda i, tab: (0, 0, 0), pipeline_mode=pl.Buffered(1)),
                pl.BlockSpec((experts, rows, hid), lambda i, tab: (0, i, 0)),
            ],
            out_specs=[
                pl.BlockSpec((experts, rows, hid), lambda i, tab: (0, i, 0)),
                pl.BlockSpec((nb, 2, tokens), lambda i, tab: (i, 0, 0)),
            ],
            scratch_shapes=[pltpu.VMEM((experts, rows, halves * half), BF)],
        ),
        out_shape=[
            jax.ShapeDtypeStruct((experts, slots, hid), BF),
            jax.ShapeDtypeStruct((blocks, 2, tokens), F32),
        ],
        compiler_params=pltpu.CompilerParams(vmem_limit_bytes=52 << 20),
        cost_estimate=pl.CostEstimate(flops=17_000_000_000, bytes_accessed=36_000_000, transcendentals=0),
        name="projected",
    )(tab, meta, tok, w, h)


def grad_kernel(nc, halves, first, tab_ref, *refs):
    picks, tok_ref, hids, rest = refs[:nc], refs[nc], refs[nc + 1 : 3 * nc + 1], refs[3 * nc + 1 :]
    if first:
        out_ref, acc_ref, sc_ref = rest
    else:
        prev_ref, out_ref, acc_ref, sc_ref, held_ref, sem, give_ref, sems = rest
        before = pltpu.make_async_copy(prev_ref, held_ref, sem)
    step, steps = pl.program_id(0), pl.num_programs(0)
    nb = picks[0].shape[1]
    group = sc_ref.shape[1] // (nc * nb * CAP)
    turn = lax.rem(step, group)
    if not first:

        @pl.when(step == 0)
        def _():
            before.start()

    for c in range(nc):
        for b in range(nb):
            at = 0
            row = pl.multiple_of((c * group + turn) * nb * CAP, CAP) + b * CAP
            for src in [tok_ref[b]] if halves == 1 else [tok_ref[b, h, c] for h in range(halves)]:
                got = jnp.dot(picks[c][0, b], src, preferred_element_type=F32).astype(BF)
                for x in range(2):
                    sc_ref[x, pl.ds(pl.multiple_of(row, CAP), CAP), at : at + src.shape[1]] = got[x * CAP : (x + 1) * CAP]
                at += src.shape[1]

    def off(rows):
        return pltpu.make_async_copy(give_ref.at[rows], out_ref.at[rows], sems.at[rows.start // 512])

    def add(place):
        for f in range(0, sc_ref.shape[2], 512):
            for x in range(2):
                hid = jnp.concatenate([hids[2 * c + x][0] for c in range(nc)], axis=0)
                got = lax.dot_general(
                    sc_ref[x, :, f : f + 512], hid, (((0,), (0,)), ((), ())), preferred_element_type=F32
                )
                place(x, slice(f, f + 512), got)

    def keep(x, rows, got):
        acc_ref[x, rows, :] = got

    def more(x, rows, got):
        acc_ref[x, rows, :] += got

    def give(x, rows, got):
        total = acc_ref[x, rows, :] + got
        if first:
            out_ref[x, rows, :] = total.astype(BF)
        else:
            give_ref[rows, x, :] = (total + held_ref[x, rows, :].astype(F32)).astype(BF)
            if x == 1:
                off(rows).start()

    @pl.when(step == group - 1)
    def _():
        add(keep)

    @pl.when((turn == group - 1) & (step > group - 1) & (step < steps - 1))
    def _():
        add(more)

    @pl.when(step == steps - 1)
    def _():
        if not first:
            before.wait()
        add(give)
        if not first:
            for f in range(0, sc_ref.shape[2], 512):
                off(slice(f, f + 512)).wait()


def grad_call(tab, pick, tok, hids, prev=None):
    blocks, tokens = pick.shape[1], pick.shape[3]
    hid = hids[0][0].shape[2]
    nc, first = len(hids), prev is None
    feats = tok.shape[3] // 2 if first else 2 * tok.shape[4]
    nb, group = (4, 2) if first else (4, 1)
    copies = (0,) if first else (1, 2, 3)
    specs = [pl.BlockSpec((1, nb, 2 * CAP, tokens), lambda i, tab, s=s: (tab[COPY + s], i, 0, 0)) for s in copies]
    args = [pick] * nc + [tok]
    if first:
        specs.append(pl.BlockSpec((nb, None, tokens, feats), lambda i, tab: (i, tab[HALF], 0, tab[COL])))
    else:
        specs.append(pl.BlockSpec((nb, 2, nc, tokens, feats // 2), lambda i, tab: (i, 0, 0, 0, 0)))
    for pair in hids:
        for x in range(2):
            at = min(x, pair[x].shape[0] - 1)
            specs.append(pl.BlockSpec((1, group * nb * CAP, hid), lambda i, tab, at=at: (at, i // group, 0)))
            args.append(pair[x])
    shape = (2, feats, hid)
    outs = shape if first else (feats, 2, hid)
    scratch = [pltpu.VMEM(shape, F32), pltpu.VMEM((2, nc * group * nb * CAP, feats), BF)]
    if not first:
        specs.append(pl.BlockSpec(memory_space=pl.ANY))
        args.append(prev)
        scratch += [pltpu.VMEM(shape, BF), pltpu.SemaphoreType.DMA]
        scratch += [pltpu.VMEM(outs, BF), pltpu.SemaphoreType.DMA((feats // 512,))]
    return pl.pallas_call(
        functools.partial(grad_kernel, nc, 1 if first else 2, first),
        grid_spec=pltpu.PrefetchScalarGridSpec(
            num_scalar_prefetch=1,
            grid=(blocks // nb,),
            in_specs=specs,
            out_specs=pl.BlockSpec(outs, lambda i, tab: (0, 0, 0), pipeline_mode=pl.Buffered(1))
            if first
            else pl.BlockSpec(memory_space=pl.ANY),
            scratch_shapes=scratch,
        ),
        out_shape=jax.ShapeDtypeStruct(outs, BF),
        compiler_params=pltpu.CompilerParams(vmem_limit_bytes=52 << 20),
        cost_estimate=pl.CostEstimate(
            flops=nc * 4_400_000_000, bytes_accessed=nc * 7_500_000 + 6_000_000, transcendentals=0
        ),
        name=f"grad_weight_{nc}",
    )(tab, *args)


def shift(x, axis, by):
    n = lax.axis_size(axis)
    return lax.ppermute(x, axis, [(i, (i + by) % n) for i in range(n)])


def body(grad_out, routes, gate_probs, hidden_saved, down_weight):
    d, e, t = lax.axis_index("dp"), lax.axis_index("expert"), lax.axis_index("etp")
    n_dp, n_ex = lax.axis_size("dp"), lax.axis_size("expert")
    tokens, half = grad_out.shape
    local, slots, hid = hidden_saved.shape[1:]
    experts = n_ex * local
    part = half // n_dp
    own = hidden_saved[0]
    tab = jnp.stack([d // 2, d % 2] + [(d - s) % n_dp for s in range(n_dp)]).astype(jnp.int32)

    tok = lax.all_gather(grad_out, ("expert", "etp"), axis=0).reshape(n_ex, 2, tokens, half)

    other = shift(grad_out, "etp", 1)
    full = jnp.where(t == 0, jnp.concatenate([grad_out, other], 1), jnp.concatenate([other, grad_out], 1))

    def slice_for(who):
        return lax.dynamic_slice(full, (0, who * (2 * part) + t * part), (tokens, part))

    cuts = [slice_for((d + s) % n_dp) for s in range(1, n_dp)]
    routes_t = routes.T
    hit = routes_t[None] == jnp.arange(experts, dtype=jnp.int32)[:, None, None]
    match = jnp.any(hit, axis=1)
    before = (jnp.arange(tokens)[:, None] < jnp.arange(tokens)[None, :]).astype(BF)
    rank = jnp.dot(match.astype(BF), before, preferred_element_type=F32)
    slot = jnp.where(match, rank, -1.0).reshape(n_ex, local, tokens)
    prob = jnp.sum(jnp.where(hit, gate_probs.T[None].astype(F32), 0.0), axis=1).reshape(n_ex, local, tokens)
    to_send = jnp.concatenate([slot, prob], axis=1)
    to_send = jnp.broadcast_to(to_send[None], (n_dp, *to_send.shape)).reshape(n_dp * n_ex, 2 * local, tokens)
    to_send, *cuts = lax.optimization_barrier((to_send, *cuts))
    meta = lax.all_to_all(to_send, ("dp", "expert"), split_axis=0, concat_axis=0)
    meta = meta.reshape(n_dp, n_ex, 2 * local, tokens)
    mine = [shift(cut, "dp", s + 1) for s, cut in enumerate(cuts)]

    own_0, own_1 = lax.optimization_barrier((own[:1], own[1:], meta, *mine))[:2]
    left_0, right_1 = shift(own_0, "dp", 1), shift(own_1, "dp", -1)
    left_1, right_0 = shift(own_1, "dp", 1), shift(own_0, "dp", -1)

    feats = lax.all_gather(jnp.stack(mine), ("expert", "etp"), axis=0).reshape(n_ex, 2, n_dp - 1, tokens, part)

    h_far = (shift(left_0, "dp", 1), shift(right_1, "dp", -1))

    pick = slots_call(meta)

    grad_hidden, scores = projected_call(tab, meta, tok, down_weight, own)
    total = grad_call(tab, pick, tok, [(own, own)])
    total = grad_call(tab, pick, feats, [(left_0, left_1), h_far, (right_0, right_1)], total)
    grad_weight = total

    back = lax.all_to_all(scores, "expert", split_axis=0, concat_axis=0)
    back = back + shift(back, "etp", 1)
    back = back.reshape(1, experts, tokens)
    numbers = jnp.arange(experts, dtype=jnp.int32)[None, :, None]
    grad_probs = jnp.sum(jnp.where(routes_t[:, None, :] == numbers, back, 0.0), axis=1).T
    return grad_hidden[None], grad_weight, grad_probs


def solution(mesh):
    placed = (
        P(("dp", "expert"), "etp"),
        P(("dp", "expert"), None),
        P(("dp", "expert"), None),
        P("dp", "expert", None, "etp"),
        P("expert", "etp", None),
    )
    return jax.shard_map(
        body,
        mesh=mesh,
        in_specs=placed,
        out_specs=(
            P("dp", "expert", None, "etp"),
            P("dp", "expert", "etp"),
            P(("dp", "expert"), None),
        ),
        check_vma=False,
    )
```

```python
import functools

import jax
import jax.numpy as jnp
from jax import lax
from jax.experimental import pallas as pl
from jax.experimental.pallas import tpu as pltpu
from jax.sharding import PartitionSpec as P

CAP = 64
BF = jnp.bfloat16
F32 = jnp.float32
HALF, COL, COPY = 0, 1, 2


def onehot_rows(slot_row, value_row):
    shape = (CAP, slot_row.shape[1])
    slots = lax.broadcasted_iota(jnp.int32, shape, 0).astype(F32)
    value = jnp.ones(shape, F32) if value_row is None else jnp.broadcast_to(value_row, shape)
    return jnp.where(jnp.broadcast_to(slot_row, shape) == slots, value, 0.0)


def slots_kernel(meta_ref, pick_ref):
    for b in range(meta_ref.shape[1]):
        for x in range(2):
            rows = onehot_rows(meta_ref[0, b, x : x + 1, :], meta_ref[0, b, 2 + x : 3 + x, :])
            pick_ref[0, b, x * CAP : (x + 1) * CAP, :] = rows.astype(BF)


def slots_call(meta):
    copies, blocks, _, tokens = meta.shape
    return pl.pallas_call(
        slots_kernel,
        grid=(copies,),
        in_specs=[pl.BlockSpec((1, blocks, 4, tokens), lambda i: (i, 0, 0, 0))],
        out_specs=pl.BlockSpec((1, blocks, 2 * CAP, tokens), lambda i: (i, 0, 0, 0)),
        out_shape=jax.ShapeDtypeStruct((copies, blocks, 2 * CAP, tokens), BF),
        cost_estimate=pl.CostEstimate(flops=10_000_000, bytes_accessed=2_500_000, transcendentals=0),
        name="slots",
    )(meta)


def projected_kernel(tab_ref, meta_ref, tok_ref, w_ref, h_ref, gh_ref, ts_ref, arr_ref):
    nb, halves, tokens, half = tok_ref.shape
    pieces = 1024
    for b in range(nb):
        rows = [onehot_rows(meta_ref[0, b, x : x + 1, :], None) for x in range(2)]
        pick = jnp.concatenate(rows, axis=0).astype(BF)
        for h in range(halves):
            for f in range(half // pieces):
                src = tok_ref[b, h, :, f * pieces : (f + 1) * pieces]
                got = jnp.dot(pick, src, preferred_element_type=F32).astype(BF)
                at = h * half + f * pieces
                for x in range(2):
                    arr_ref[x, b * CAP : (b + 1) * CAP, at : at + pieces] = got[x * CAP : (x + 1) * CAP]
    for x in range(2):
        proj = lax.dot_general(arr_ref[x], w_ref[x], (((1,), (1,)), ((), ())), preferred_element_type=F32)
        for b in range(nb):
            slot_row = meta_ref[0, b, x : x + 1, :]
            ones = onehot_rows(slot_row, None)
            weights = onehot_rows(slot_row, meta_ref[0, b, 2 + x : 3 + x, :])
            prob = jnp.sum(weights, axis=1, keepdims=True)
            mine = proj[b * CAP : (b + 1) * CAP]
            gh_ref[x, b * CAP : (b + 1) * CAP, :] = (prob * mine).astype(BF)
            score = jnp.sum(h_ref[x, b * CAP : (b + 1) * CAP, :].astype(F32) * mine, axis=1, keepdims=True)
            ts_ref[b, x : x + 1, :] = jnp.sum(ones * score, axis=0, keepdims=True)


def projected_call(tab, meta, tok, w, h):
    blocks, halves, tokens, half = tok.shape
    experts, slots, hid = h.shape
    nb = 4
    rows = nb * CAP
    return pl.pallas_call(
        projected_kernel,
        grid_spec=pltpu.PrefetchScalarGridSpec(
            num_scalar_prefetch=1,
            grid=(blocks // nb,),
            in_specs=[
                pl.BlockSpec((1, nb, 4, tokens), lambda i, tab: (tab[COPY], i, 0, 0)),
                pl.BlockSpec((nb, halves, tokens, half), lambda i, tab: (i, 0, 0, 0)),
                pl.BlockSpec(w.shape, lambda i, tab: (0, 0, 0), pipeline_mode=pl.Buffered(1)),
                pl.BlockSpec((experts, rows, hid), lambda i, tab: (0, i, 0)),
            ],
            out_specs=[
                pl.BlockSpec((experts, rows, hid), lambda i, tab: (0, i, 0)),
                pl.BlockSpec((nb, 2, tokens), lambda i, tab: (i, 0, 0)),
            ],
            scratch_shapes=[pltpu.VMEM((experts, rows, halves * half), BF)],
        ),
        out_shape=[
            jax.ShapeDtypeStruct((experts, slots, hid), BF),
            jax.ShapeDtypeStruct((blocks, 2, tokens), F32),
        ],
        compiler_params=pltpu.CompilerParams(vmem_limit_bytes=52 << 20),
        cost_estimate=pl.CostEstimate(flops=17_000_000_000, bytes_accessed=36_000_000, transcendentals=0),
        name="projected",
    )(tab, meta, tok, w, h)


def grad_kernel(nc, halves, first, tab_ref, *refs):
    picks, tok_ref, hids, rest = refs[:nc], refs[nc], refs[nc + 1 : 3 * nc + 1], refs[3 * nc + 1 :]
    if first:
        out_ref, acc_ref, sc_ref = rest
    else:
        prev_ref, out_ref, acc_ref, sc_ref, held_ref, sem, give_ref, sems = rest
        before = pltpu.make_async_copy(prev_ref, held_ref, sem)
    step, steps = pl.program_id(0), pl.num_programs(0)
    nb = picks[0].shape[1]
    group = sc_ref.shape[1] // (nc * nb * CAP)
    turn = lax.rem(step, group)
    if not first:

        @pl.when(step == 0)
        def _():
            before.start()

    for c in range(nc):
        for b in range(nb):
            at = 0
            row = (c * nb + b) * CAP
            for src in [tok_ref[b]] if halves == 1 else [tok_ref[b, h, c] for h in range(halves)]:
                got = jnp.dot(picks[c][0, b], src, preferred_element_type=F32).astype(BF)
                for x in range(2):
                    sc_ref[x, row : row + CAP, at : at + src.shape[1]] = got[x * CAP : (x + 1) * CAP]
                at += src.shape[1]

    def off(rows):
        return pltpu.make_async_copy(give_ref.at[rows], out_ref.at[rows], sems.at[rows.start // 512])

    def add(place):
        for f in range(0, sc_ref.shape[2], 512):
            for x in range(2):
                hid = jnp.concatenate([hids[2 * c + x][0] for c in range(nc)], axis=0)
                got = lax.dot_general(
                    sc_ref[x, :, f : f + 512], hid, (((0,), (0,)), ((), ())), preferred_element_type=F32
                )
                place(x, slice(f, f + 512), got)

    def keep(x, rows, got):
        acc_ref[x, rows, :] = got

    def more(x, rows, got):
        acc_ref[x, rows, :] += got

    def give(x, rows, got):
        total = acc_ref[x, rows, :] + got
        if first:
            out_ref[x, rows, :] = total.astype(BF)
        else:
            give_ref[rows, x, :] = (total + held_ref[x, rows, :].astype(F32)).astype(BF)
            if x == 1:
                off(rows).start()

    @pl.when(step == group - 1)
    def _():
        add(keep)

    @pl.when((turn == group - 1) & (step > group - 1) & (step < steps - 1))
    def _():
        add(more)

    @pl.when(step == steps - 1)
    def _():
        if not first:
            before.wait()
        add(give)
        if not first:
            for f in range(0, sc_ref.shape[2], 512):
                off(slice(f, f + 512)).wait()


def grad_call(tab, pick, tok, hids, prev=None):
    blocks, tokens = pick.shape[1], pick.shape[3]
    hid = hids[0][0].shape[2]
    nc, first = len(hids), prev is None
    feats = tok.shape[3] // 2 if first else 2 * tok.shape[4]
    nb, group = (8, 1) if first else (4, 1)
    copies = (0,) if first else (1, 2, 3)
    specs = [pl.BlockSpec((1, nb, 2 * CAP, tokens), lambda i, tab, s=s: (tab[COPY + s], i, 0, 0)) for s in copies]
    args = [pick] * nc + [tok]
    if first:
        specs.append(pl.BlockSpec((nb, None, tokens, feats), lambda i, tab: (i, tab[HALF], 0, tab[COL])))
    else:
        specs.append(pl.BlockSpec((nb, 2, nc, tokens, feats // 2), lambda i, tab: (i, 0, 0, 0, 0)))
    for pair in hids:
        for x in range(2):
            at = min(x, pair[x].shape[0] - 1)
            specs.append(pl.BlockSpec((1, group * nb * CAP, hid), lambda i, tab, at=at: (at, i // group, 0)))
            args.append(pair[x])
    shape = (2, feats, hid)
    outs = shape if first else (feats, 2, hid)
    scratch = [pltpu.VMEM(shape, F32), pltpu.VMEM((2, nc * group * nb * CAP, feats), BF)]
    if not first:
        specs.append(pl.BlockSpec(memory_space=pl.ANY))
        args.append(prev)
        scratch += [pltpu.VMEM(shape, BF), pltpu.SemaphoreType.DMA]
        scratch += [pltpu.VMEM(outs, BF), pltpu.SemaphoreType.DMA((feats // 512,))]
    return pl.pallas_call(
        functools.partial(grad_kernel, nc, 1 if first else 2, first),
        grid_spec=pltpu.PrefetchScalarGridSpec(
            num_scalar_prefetch=1,
            grid=(blocks // nb,),
            in_specs=specs,
            out_specs=pl.BlockSpec(outs, lambda i, tab: (0, 0, 0), pipeline_mode=pl.Buffered(1))
            if first
            else pl.BlockSpec(memory_space=pl.ANY),
            scratch_shapes=scratch,
        ),
        out_shape=jax.ShapeDtypeStruct(outs, BF),
        compiler_params=pltpu.CompilerParams(vmem_limit_bytes=52 << 20),
        cost_estimate=pl.CostEstimate(
            flops=nc * 4_400_000_000, bytes_accessed=nc * 7_500_000 + 6_000_000, transcendentals=0
        ),
        name=f"grad_weight_{nc}",
    )(tab, *args)


def shift(x, axis, by):
    n = lax.axis_size(axis)
    return lax.ppermute(x, axis, [(i, (i + by) % n) for i in range(n)])


def body(grad_out, routes, gate_probs, hidden_saved, down_weight):
    d, e, t = lax.axis_index("dp"), lax.axis_index("expert"), lax.axis_index("etp")
    n_dp, n_ex = lax.axis_size("dp"), lax.axis_size("expert")
    tokens, half = grad_out.shape
    local, slots, hid = hidden_saved.shape[1:]
    experts = n_ex * local
    part = half // n_dp
    own = hidden_saved[0]
    tab = jnp.stack([d // 2, d % 2] + [(d - s) % n_dp for s in range(n_dp)]).astype(jnp.int32)

    tok = lax.all_gather(grad_out, ("expert", "etp"), axis=0).reshape(n_ex, 2, tokens, half)

    other = shift(grad_out, "etp", 1)
    full = jnp.where(t == 0, jnp.concatenate([grad_out, other], 1), jnp.concatenate([other, grad_out], 1))

    def slice_for(who):
        return lax.dynamic_slice(full, (0, who * (2 * part) + t * part), (tokens, part))

    cuts = [slice_for((d + s) % n_dp) for s in range(1, n_dp)]
    routes_t = routes.T
    hit = routes_t[None] == jnp.arange(experts, dtype=jnp.int32)[:, None, None]
    match = jnp.any(hit, axis=1)
    before = (jnp.arange(tokens)[:, None] < jnp.arange(tokens)[None, :]).astype(BF)
    rank = jnp.dot(match.astype(BF), before, preferred_element_type=F32)
    slot = jnp.where(match, rank, -1.0).reshape(n_ex, local, tokens)
    prob = jnp.sum(jnp.where(hit, gate_probs.T[None].astype(F32), 0.0), axis=1).reshape(n_ex, local, tokens)
    to_send = jnp.concatenate([slot, prob], axis=1)
    to_send = jnp.broadcast_to(to_send[None], (n_dp, *to_send.shape)).reshape(n_dp * n_ex, 2 * local, tokens)
    to_send, *cuts = lax.optimization_barrier((to_send, *cuts))
    meta = lax.all_to_all(to_send, ("dp", "expert"), split_axis=0, concat_axis=0)
    meta = meta.reshape(n_dp, n_ex, 2 * local, tokens)
    mine = [shift(cut, "dp", s + 1) for s, cut in enumerate(cuts)]

    own_0, own_1 = lax.optimization_barrier((own[:1], own[1:], meta, *mine))[:2]
    left_0, right_1 = shift(own_0, "dp", 1), shift(own_1, "dp", -1)
    left_1, right_0 = shift(own_1, "dp", 1), shift(own_0, "dp", -1)

    feats = lax.all_gather(jnp.stack(mine), ("expert", "etp"), axis=0).reshape(n_ex, 2, n_dp - 1, tokens, part)

    h_far = (shift(left_0, "dp", 1), shift(right_1, "dp", -1))

    pick = slots_call(meta)

    grad_hidden, scores = projected_call(tab, meta, tok, down_weight, own)
    total = grad_call(tab, pick, tok, [(own, own)])
    total = grad_call(tab, pick, feats, [(left_0, left_1), h_far, (right_0, right_1)], total)
    grad_weight = total

    back = lax.all_to_all(scores, "expert", split_axis=0, concat_axis=0)
    back = back + shift(back, "etp", 1)
    back = back.reshape(1, experts, tokens)
    numbers = jnp.arange(experts, dtype=jnp.int32)[None, :, None]
    grad_probs = jnp.sum(jnp.where(routes_t[:, None, :] == numbers, back, 0.0), axis=1).T
    return grad_hidden[None], grad_weight, grad_probs


def solution(mesh):
    placed = (
        P(("dp", "expert"), "etp"),
        P(("dp", "expert"), None),
        P(("dp", "expert"), None),
        P("dp", "expert", None, "etp"),
        P("expert", "etp", None),
    )
    return jax.shard_map(
        body,
        mesh=mesh,
        in_specs=placed,
        out_specs=(
            P("dp", "expert", None, "etp"),
            P("dp", "expert", "etp"),
            P(("dp", "expert"), None),
        ),
        check_vma=False,
    )
```
